32 devices in a mesh: seq: 4 (over x, core), head: 8 (over z, y).
Axes of the slice: x: 2, y: 2, z: 4, core: 2. Of those that a mesh axis runs over, the one named last changes fastest.
Arguments:
- inner_input: bfloat16 [2048, 16384], P('seq', 'head'), may hold values from -6 to 6
- gate_input: bfloat16 [2048, 16384], P('seq', 'head'), may hold values from -48 to 48
- bc_input: bfloat16 [2048, 4096], P('seq'), may hold values from -6 to 6
- dt_input: float32 [256, 2048], P('head', 'seq'), may hold values from -11.5 to 0
- log_rate: float32 [256], P('head'), may hold values from -1.2 to 0
- skip_weight: float32 [256], P('head'), may hold values from 0.5 to 1.5
- conv_weight_x: float32 [4, 16384], P(None, 'head'), may hold values from -3 to 3
- conv_bias_x: float32 [16384], P('head'), may hold values from -3 to 3
- conv_weight_bc: float32 [4, 4096], replicated, may hold values from -3 to 3
- conv_bias_bc: float32 [4096], replicated, may hold values from -3 to 3
- conv_tail_x: bfloat16 [3, 16384], P(None, 'head'), may hold values from -6 to 6
- conv_tail_bc: bfloat16 [3, 4096], replicated, may hold values from -6 to 6
- init_state: float32 [256, 64, 256], P('head'), may hold values from -0.6 to 0.6
- norm_gain: float32 [16384], P('head'), may hold values from 0.5 to 1.5
- out_weight: bfloat16 [16384, 8192], P('head', 'seq'), may hold values from -0.046875 to 0.046875
Outputs:
- layer_out: bfloat16 [2048, 8192], P(('seq', 'head'))
- boundary_states: float32 [4, 256, 64, 256], P('seq', 'head')
The draws below stay inside these ranges and needn't reach their ends.
All inputs are finite; a program needn't handle non-finite values.
Results may differ from the reference program's by a relative error of at most 0.015.
Values may be sent and summed in bfloat16 or wider, within the bound.
A program may use at most 192 MiB of HBM per device.

```python
import jax
import jax.numpy as jnp
from jax import lax

D = 8192
MIXER_HEADS = 256
HEADDIM = 64
STATE = 256
GROUPS = 8
KERNEL = 4
SPAN = 128
TOK_SEQ = 512
DINNER = 16384
TOKEN_COUNT = 2048
N_SEQ = 4
N_HEAD = 8


def draw_dt_input(key, part):
    random_keys = jax.random.split(key, 4)
    gradual_span = jax.random.randint(random_keys[0], (MIXER_HEADS, 1), 0, 10) < 5
    rough = jnp.exp(jax.random.uniform(random_keys[1], (MIXER_HEADS, TOKEN_COUNT), minval=-0.5, maxval=0.5))
    gradual_step = 0.5 / TOKEN_COUNT * rough
    rapid_step = 0.04 * rough
    locations = jax.random.randint(random_keys[2], (3,), 0, TOKEN_COUNT)
    quick_span = jnp.any(jnp.arange(TOKEN_COUNT)[:, None] == locations[None, :], axis=1)
    quick_span_step = jax.random.uniform(random_keys[3], (MIXER_HEADS, TOKEN_COUNT), minval=0.25, maxval=0.6)
    stride_length = jnp.where(quick_span[None, :], quick_span_step, jnp.where(gradual_span, gradual_step, rapid_step))
    return jnp.log(jnp.expm1(stride_length)).astype(jnp.float32)


def draw_gate_input(key, part):
    random_keys = jax.random.split(key, 3)
    trend = jnp.exp(jnp.log(3.0) * jnp.arange(DINNER) / DINNER)[None, :]
    column_scale = jnp.exp(jax.random.uniform(random_keys[0], (1, DINNER), minval=-1.15, maxval=1.15)) * trend
    row_scale = jnp.exp(jax.random.uniform(random_keys[1], (TOKEN_COUNT, 1), minval=-1.15, maxval=1.15))
    base = jnp.clip(jax.random.normal(random_keys[2], (TOKEN_COUNT, DINNER)), -4.0, 4.0)
    return (0.25 * base * column_scale * row_scale).astype(jnp.bfloat16)


def steps_of(key, dims, cuts, smallest, high):
    level = 1.0
    for position, parts in cuts:
        steps = jax.random.uniform(jax.random.fold_in(jax.random.fold_in(key, 6), position), (parts,), jnp.float32, smallest / len(cuts), high / len(cuts))
        level = level * jnp.repeat(jnp.exp(steps), dims[position] // parts).reshape((-1,) + (1,) * (len(dims) - 1 - position))
    return level


def noise(own_key, dims, deviation, bound, pieces=(), kind=jnp.bfloat16):
    level = steps_of(own_key, dims, pieces, -0.22, 0.18) if pieces else 1.0
    result = jax.random.normal(own_key, dims, jnp.float32) * deviation * level
    return jnp.minimum(jnp.maximum(result, -bound), bound).astype(kind)


def setup_inputs(seed: int = 0) -> dict:
    keys = jax.random.split(jax.random.key(seed), 16)
    inner_input = noise(keys[0], (TOKEN_COUNT, DINNER), 1.0, 6.0, ((0, 4), (1, 8)))
    gate_input = draw_gate_input(jax.random.fold_in(keys[15], 71), 0)
    bc_input = noise(keys[2], (TOKEN_COUNT, 2 * GROUPS * STATE), 1.0, 6.0, ((0, 4),))
    dt_input = draw_dt_input(jax.random.fold_in(keys[15], 71), 0)
    log_rate = jnp.clip(-1.2 + 1.2 * jax.random.uniform(keys[4], (MIXER_HEADS,), jnp.float32) ** steps_of(keys[4], (MIXER_HEADS,), ((0, 8),), -0.2, 0.2), -1.2, 0.0)
    skip_weight = jnp.clip(0.5 + 1.0 * jax.random.uniform(keys[5], (MIXER_HEADS,), jnp.float32) ** steps_of(keys[5], (MIXER_HEADS,), ((0, 8),), -0.2, 0.2), 0.5, 1.5)
    conv_weight_x = noise(keys[6], (KERNEL, DINNER), 0.5, 3.0, ((1, 8),), jnp.float32)
    conv_bias_x = noise(keys[7], (DINNER,), 0.5, 3.0, ((0, 8),), jnp.float32)
    conv_weight_bc = noise(keys[8], (KERNEL, 2 * GROUPS * STATE), 0.5, 3.0, (), jnp.float32)
    conv_bias_bc = noise(keys[9], (2 * GROUPS * STATE,), 0.5, 3.0, (), jnp.float32)
    conv_tail_x = noise(keys[10], (KERNEL - 1, DINNER), 1.0, 6.0, ((1, 8),))
    conv_tail_bc = noise(keys[11], (KERNEL - 1, 2 * GROUPS * STATE), 1.0, 6.0)
    init_state = noise(keys[12], (MIXER_HEADS, HEADDIM, STATE), 0.1, 0.6, ((0, 8),), jnp.float32)
    norm_gain = jnp.clip(1.0 + 0.1 * jax.random.normal(keys[13], (DINNER,), jnp.float32), 0.5, 1.5)
    out_weight = noise(keys[14], (DINNER, D), DINNER ** -0.5, 0.046875, ((0, 8), (1, 4)))
    return dict(inner_input=inner_input, gate_input=gate_input, bc_input=bc_input, dt_input=dt_input, log_rate=log_rate, skip_weight=skip_weight, conv_weight_x=conv_weight_x, conv_bias_x=conv_bias_x, conv_weight_bc=conv_weight_bc, conv_bias_bc=conv_bias_bc, conv_tail_x=conv_tail_x, conv_tail_bc=conv_tail_bc, init_state=init_state, norm_gain=norm_gain, out_weight=out_weight)


highest = lax.Precision.HIGHEST
norm_eps = 1e-05

def causal_conv(values, previous, kernel_weight, kernel_bias):
    extended = jnp.concatenate([previous, values], axis=0)
    length = values.shape[0]
    running = jnp.zeros_like(values) + kernel_bias[None, :]
    for offset in range(KERNEL):
        running = running + kernel_weight[offset][None, :] * extended[offset:offset + length]
    return running

def ssd_block(span_x, span_b, span_c, span_step, span_log, state):
    cumul = jnp.cumsum(span_log, axis=1)
    length = span_x.shape[0]
    causal = (jnp.arange(length)[:, None] >= jnp.arange(length)[None, :])[None]
    spread = jnp.where(causal, cumul[:, :, None] - cumul[:, None, :], 0.0)
    decays = jnp.where(causal, jnp.exp(spread), 0.0)
    scores = jnp.einsum('thn,shn->hts', span_c, span_b, precision=highest)
    mixer = scores * decays * span_step[:, None, :]
    output = jnp.einsum('hts,shp->thp', mixer, span_x, precision=highest)
    carried = jnp.einsum('thn,hpn->thp', span_c, state, precision=highest)
    output = output + jnp.exp(cumul).T[:, :, None] * carried
    weights = jnp.exp(cumul[:, -1:] - cumul) * span_step
    written = jnp.einsum('hs,shp,shn->hpn', weights, span_x, span_b, precision=highest)
    new_state = jnp.exp(cumul[:, -1])[:, None, None] * state + written
    return (output, new_state)

def reference(inner_input, gate_input, bc_input, dt_input, log_rate, skip_weight, conv_weight_x, conv_bias_x, conv_weight_bc, conv_bias_bc, conv_tail_x, conv_tail_bc, init_state, norm_gain, out_weight):
    conv_x = jax.nn.silu(causal_conv(inner_input.astype(jnp.float32), conv_tail_x.astype(jnp.float32), conv_weight_x, conv_bias_x)).astype(jnp.bfloat16)
    conv_bc = jax.nn.silu(causal_conv(bc_input.astype(jnp.float32), conv_tail_bc.astype(jnp.float32), conv_weight_bc, conv_bias_bc)).astype(jnp.bfloat16)
    stride_length = jax.nn.softplus(dt_input)
    decay_log = -jnp.exp(log_rate)[:, None] * stride_length
    per_group = MIXER_HEADS // GROUPS
    spans_group = TOK_SEQ // SPAN

    def span_body(state, span_index):
        first_row = (span_index * SPAN).astype(jnp.int32)
        span_x = lax.dynamic_slice_in_dim(conv_x, first_row, SPAN, 0).astype(jnp.float32).reshape(SPAN, MIXER_HEADS, HEADDIM)
        span_bc = lax.dynamic_slice_in_dim(conv_bc, first_row, SPAN, 0).astype(jnp.float32)
        span_b = jnp.repeat(span_bc[:, :GROUPS * STATE].reshape(SPAN, GROUPS, STATE), per_group, axis=1)
        span_c = jnp.repeat(span_bc[:, GROUPS * STATE:].reshape(SPAN, GROUPS, STATE), per_group, axis=1)
        span_step = lax.dynamic_slice_in_dim(stride_length, first_row, SPAN, 1)
        span_log = lax.dynamic_slice_in_dim(decay_log, first_row, SPAN, 1)
        output, new_state = ssd_block(span_x, span_b, span_c, span_step, span_log, state)
        output = output + skip_weight[None, :, None] * span_x
        return (new_state, output)

    def group_body(state, group_index):
        indices = group_index * spans_group + jnp.arange(spans_group, dtype=jnp.int32)
        state, outputs = lax.scan(span_body, state, indices)
        return (state, (state, outputs))
    final_state, (boundary_states, outputs) = lax.scan(group_body, init_state, jnp.arange(N_SEQ, dtype=jnp.int32))
    mixed = outputs.reshape(TOKEN_COUNT, DINNER) * jax.nn.silu(gate_input.astype(jnp.float32))
    grouped = mixed.reshape(TOKEN_COUNT, GROUPS, DINNER // GROUPS)
    mean_square = lax.optimization_barrier(jnp.mean(grouped * grouped, axis=2, keepdims=True))
    normed = ((grouped * lax.rsqrt(mean_square + norm_eps)).reshape(TOKEN_COUNT, DINNER) * norm_gain[None, :]).astype(jnp.bfloat16)
    block_width = DINNER // N_HEAD

    def add_block(counter, running):
        offset = (counter * block_width).astype(jnp.int32)
        block_rows = lax.dynamic_slice_in_dim(normed, offset, block_width, 1)
        block_weight = lax.dynamic_slice_in_dim(out_weight, offset, block_width, 0)
        partial_sum = jnp.dot(block_rows, block_weight, preferred_element_type=jnp.float32).astype(jnp.bfloat16)
        return running + lax.optimization_barrier(partial_sum).astype(jnp.float32)
    layer_out = lax.fori_loop(0, N_HEAD, add_block, jnp.zeros((TOKEN_COUNT, D), jnp.float32)).astype(jnp.bfloat16)
    return (layer_out, boundary_states)
```

```python
import functools

import jax
import jax.numpy as jnp
from jax import lax
from jax.experimental import pallas as pl
from jax.experimental.pallas import tpu as pltpu
from jax.sharding import PartitionSpec as P

MIXER_HEADS = 256
HEADDIM = 64
STATE = 256
GROUPS = 8
KERNEL = 4
SPAN = 128
DINNER = 16384
EXTRA = 16
VMEM_LIMIT = 48 * 1024 * 1024

highest = lax.Precision.HIGHEST
norm_eps = 1e-05
f32 = jnp.float32
bf16 = jnp.bfloat16


def silu(v):
    return v * (1.0 / (1.0 + jnp.exp(-v)))


def shifted(cur, prev8, by):
    moved = pltpu.roll(cur, by, 0)
    before = pltpu.roll(prev8, by, 0)
    row = lax.broadcasted_iota(jnp.int32, before.shape, 0)
    first = jnp.where(row < by, before, moved[:8])
    return jnp.concatenate([first, moved[8:]], axis=0)


def conv_block(in_ref, prev_ref, w_ref, b_ref, out_ref, chunk):
    width = in_ref.shape[1]
    rows = in_ref.shape[0]
    for c in range(0, width, chunk):
        cols = slice(c, c + chunk)
        cur = in_ref[:, cols].astype(f32)
        prev8 = prev_ref[:, cols]
        total = b_ref[:, cols] + w_ref[KERNEL - 1 : KERNEL, cols] * cur
        for by in range(1, KERNEL):
            k = KERNEL - 1 - by
            total = total + w_ref[k : k + 1, cols] * shifted(cur, prev8, by)
        prev_ref[:, cols] = cur[rows - 8 :]
        out_ref[:, cols] = silu(total).astype(bf16)


def spread_matrix(heads):
    h = lax.broadcasted_iota(jnp.int32, (heads, heads * HEADDIM), 0)
    c = lax.broadcasted_iota(jnp.int32, (heads, heads * HEADDIM), 1)
    return jnp.where(c // HEADDIM == h, 1.0, 0.0).astype(f32)


def spread(values, matrix):
    return jnp.dot(values, matrix, precision=highest, preferred_element_type=f32)


def softplus(v):
    e = jnp.exp(-jnp.abs(v))
    u = 1.0 + e
    series = e * (1.0 - e * (0.5 - e * (1.0 / 3.0 - 0.25 * e)))
    return jnp.maximum(v, 0.0) + jnp.where(e < 0.015625, series, jnp.log(u))


def transposed_dot(lhs, rhs):
    return lax.dot_general(
        lhs, rhs, (((1,), (1,)), ((), ())), precision=highest, preferred_element_type=f32
    )


def decay_terms(dt_ref, rate_ref):
    step = softplus(dt_ref[...])
    log = -jnp.exp(rate_ref[...]) * step
    t = lax.broadcasted_iota(jnp.int32, (SPAN, SPAN), 0)
    s = lax.broadcasted_iota(jnp.int32, (SPAN, SPAN), 1)
    lower = jnp.where(t >= s, 1.0, 0.0).astype(f32)
    eye = jnp.where(t == s, 1.0, 0.0).astype(f32)
    cumul_row = transposed_dot(log, lower)
    cumul_col = transposed_dot(lower, log)
    step_col = transposed_dot(eye, step)
    return step, step_col, cumul_row, cumul_col, t >= s


def state_kernel(
    g_ref, inner, bin_, cin, dt, rate, wx, bx, wb, wc, bb, bc, halo_x, halo_b, halo_c,
    x_out, b_out, c_out, enter_out, send_out, local_out,
    prev_x, prev_b, prev_c, state, total,
):
    i = pl.program_id(0)
    heads = dt.shape[0]

    @pl.when(i == 0)
    def _():
        prev_x[...] = halo_x[...].astype(f32)
        prev_b[...] = halo_b[...].astype(f32)
        prev_c[...] = halo_c[...].astype(f32)
        state[...] = jnp.zeros_like(state)
        total[...] = jnp.zeros_like(total)

    conv_block(inner, prev_x, wx, bx, x_out, 256)
    conv_block(bin_, prev_b, wb, bb, b_out, 256)
    conv_block(cin, prev_c, wc, bc, c_out, 256)
    step, step_col, cumul_row, cumul_col, causal = decay_terms(dt, rate)
    last = cumul_col[SPAN - 1 :]
    matrix = spread_matrix(heads)
    weights = spread(jnp.exp(last - cumul_col) * step_col, matrix)
    last8 = spread(jnp.broadcast_to(last, (8, heads)), matrix)
    enter_out[0] = state[...].astype(bf16)
    weighted = (x_out[...].astype(f32) * weights).astype(bf16)
    b_t = b_out[...].astype(f32).T.astype(bf16)
    written = jnp.dot(b_t, weighted, preferred_element_type=f32)
    state[...] = jnp.exp(last8[:1]) * state[...] + written
    total[...] += last8

    @pl.when(i == pl.num_programs(0) - 1)
    def _():
        local_out[...] = state[...]
        send_out[:STATE] = state[...].astype(bf16)
        tl = total[:1]
        high = tl.astype(bf16).astype(f32)
        row = lax.broadcasted_iota(jnp.int32, (EXTRA, tl.shape[1]), 0)
        send_out[STATE:] = jnp.where(row == 0, high, jnp.where(row == 1, tl - high, 0.0)).astype(bf16)


def local_kernel(x, b, c, dt, rate, skip, enter, y_out):
    heads = dt.shape[0]
    step, step_col, cumul_row, cumul_col, causal = decay_terms(dt, rate)
    matrix = spread_matrix(heads)
    scores = lax.dot_general(
        c[...], b[...], (((1,), (1,)), ((), ())), preferred_element_type=f32
    )
    row_term = jnp.log(step) - cumul_row
    growth = spread(jnp.exp(cumul_col), matrix)
    skip_row = spread(jnp.broadcast_to(skip[...], (8, heads)), matrix)[:1]
    lane = lax.broadcasted_iota(jnp.int32, (SPAN, 2 * HEADDIM), 1)
    zero = jnp.zeros((SPAN, 2 * HEADDIM), bf16)
    for pair in range(heads // 2):
        cols = slice(pair * 2 * HEADDIM, (pair + 1) * 2 * HEADDIM)
        mixers = []
        for h in (2 * pair, 2 * pair + 1):
            power = jnp.where(causal, cumul_col[:, h : h + 1] + row_term[h : h + 1], -1e30)
            mixers.append((scores * jnp.exp(power)).astype(bf16))
        xp = x[:, cols]
        both = jnp.concatenate(
            [jnp.where(lane < HEADDIM, xp, zero), jnp.where(lane >= HEADDIM, xp, zero)], axis=0
        )
        inside = jnp.dot(
            jnp.concatenate(mixers, axis=1), both, preferred_element_type=f32
        )
        carried = jnp.dot(c[...], enter[0, :, cols], preferred_element_type=f32)
        y_out[:, cols] = (
            inside + growth[:, cols] * carried + skip_row[:, cols] * xp.astype(f32)
        )


def output_kernel(
    meta, y, c, gate, dt, rate, gain, gathered, init, local, normed_out, boundary_out,
    incoming, entering, mixed, offset, *, block, whole_group,
):
    i = pl.program_id(0)
    heads = dt.shape[0]
    width = y.shape[1]
    count = gathered.shape[0]

    @pl.when(i == 0)
    def _():
        place = meta[0]
        rate_sum = jnp.zeros((1, width), f32)
        incoming[...] = jnp.zeros_like(incoming)
        for k in range(count - 2, -1, -1):
            live = k < place
            tail = gathered[k, STATE:].astype(f32)
            factor = jnp.where(live, jnp.exp(rate_sum), 0.0)
            incoming[...] += factor * gathered[k, :STATE].astype(f32)
            rate_sum = rate_sum + jnp.where(live, tail[0:1] + tail[1:2], 0.0)
        tail = gathered[place, STATE:].astype(f32)
        own = jnp.exp(tail[0:1] + tail[1:2])
        for k in range(0, width, 256):
            cols = slice(k, k + 256)
            value = incoming[:, cols] + jnp.exp(rate_sum[:, cols]) * init[cols, :].T
            entering[:, cols] = value.astype(bf16)
            boundary_out[cols, :] = (own[:, cols] * value + local[:, cols]).T
        offset[...] = jnp.zeros_like(offset)

    step, step_col, cumul_row, cumul_col, causal = decay_terms(dt, rate)
    cumul_col = cumul_col + offset[:1]
    offset[...] = jnp.broadcast_to(cumul_col[SPAN - 1 :], offset.shape)
    growth = spread(jnp.exp(cumul_col), spread_matrix(heads))
    squares = jnp.zeros((SPAN, 1), f32)
    for k in range(0, width, 256):
        cols = slice(k, k + 256)
        carried = jnp.dot(c[...], entering[:, cols], preferred_element_type=f32)
        value = (y[:, cols] + growth[:, cols] * carried) * silu(gate[:, cols].astype(f32))
        mixed[:, cols] = value
        squares = squares + jnp.sum(value * value, axis=1, keepdims=True)
    if whole_group:
        inverse = lax.rsqrt(squares / width + norm_eps)
    for q in range(SPAN // block):
        rows = slice(q * block, (q + 1) * block)
        place = pl.multiple_of(meta[1 + i * (SPAN // block) + q], block)
        value = mixed[rows, :]
        if whole_group:
            value = value * inverse[rows] * gain[...]
        normed_out[pl.ds(place, block), :] = value.astype(normed_out.dtype)


def params():
    return pltpu.CompilerParams(vmem_limit_bytes=VMEM_LIMIT)


def body(
    inner_input,
    gate_input,
    bc_input,
    dt_input,
    log_rate,
    skip_weight,
    conv_weight_x,
    conv_bias_x,
    conv_weight_bc,
    conv_bias_bc,
    conv_tail_x,
    conv_tail_bc,
    init_state,
    norm_gain,
    out_weight,
):
    seq_count = lax.axis_size("seq")
    head_count = lax.axis_size("head")
    seq_index = lax.axis_index("seq")
    head_index = lax.axis_index("head")
    rows, width = inner_input.shape
    heads = dt_input.shape[0]
    per_group = MIXER_HEADS // GROUPS
    group = (head_index * heads // per_group).astype(jnp.int32)
    spans = rows // SPAN
    block = rows // head_count
    group_width = DINNER // GROUPS
    whole_group = width == group_width

    other_core = lax.ppermute(out_weight, "seq", [(i, i ^ 1) for i in range(seq_count)])

    def pair_columns(table, axis):
        return [
            lax.dynamic_slice_in_dim(table, (g + group) * STATE, STATE, axis) for g in (0, GROUPS)
        ]

    tail_rows = rows - KERNEL + 1
    last_rows = jnp.concatenate(
        [inner_input[tail_rows:]] + pair_columns(bc_input[tail_rows:], 1), axis=1
    )
    arrived = lax.ppermute(last_rows, "seq", [(i, i + 1) for i in range(seq_count - 1)])
    first_rows = jnp.concatenate([conv_tail_x] + pair_columns(conv_tail_bc, 1), axis=1)
    halo = jnp.where(seq_index == 0, first_rows, arrived)
    halo = jnp.pad(halo, ((8 - KERNEL + 1, 0), (0, 0)))
    rate = log_rate[:, None]

    def const(shape, *index):
        return pl.BlockSpec(shape, lambda i, *_: index)

    span_x = pl.BlockSpec((SPAN, width), lambda i, *_: (i, 0))
    span_bc = pl.BlockSpec((SPAN, STATE), lambda i, *_: (i, 0))
    span_dt = pl.BlockSpec((heads, SPAN), lambda i, *_: (0, i))

    conv_x, conv_b, conv_c, enter, sent, local = pl.pallas_call(
        state_kernel,
        grid_spec=pltpu.PrefetchScalarGridSpec(
            num_scalar_prefetch=1,
            grid=(spans,),
            in_specs=[
                span_x,
                pl.BlockSpec((SPAN, STATE), lambda i, g: (i, g[0])),
                pl.BlockSpec((SPAN, STATE), lambda i, g: (i, g[0] + GROUPS)),
                span_dt,
                const((heads, 1), 0, 0),
                const((KERNEL, width), 0, 0),
                const((1, width), 0, 0),
                pl.BlockSpec((KERNEL, STATE), lambda i, g: (0, g[0])),
                pl.BlockSpec((KERNEL, STATE), lambda i, g: (0, g[0] + GROUPS)),
                pl.BlockSpec((1, STATE), lambda i, g: (0, g[0])),
                pl.BlockSpec((1, STATE), lambda i, g: (0, g[0] + GROUPS)),
                const((8, width), 0, 0),
                const((8, STATE), 0, width // STATE),
                const((8, STATE), 0, width // STATE + 1),
            ],
            out_specs=[
                span_x,
                span_bc,
                span_bc,
                pl.BlockSpec((1, STATE, width), lambda i, *_: (i, 0, 0)),
                const((STATE + EXTRA, width), 0, 0),
                const((STATE, width), 0, 0),
            ],
            scratch_shapes=[
                pltpu.VMEM((8, width), f32),
                pltpu.VMEM((8, STATE), f32),
                pltpu.VMEM((8, STATE), f32),
                pltpu.VMEM((STATE, width), f32),
                pltpu.VMEM((8, width), f32),
            ],
        ),
        out_shape=[
            jax.ShapeDtypeStruct((rows, width), bf16),
            jax.ShapeDtypeStruct((rows, STATE), bf16),
            jax.ShapeDtypeStruct((rows, STATE), bf16),
            jax.ShapeDtypeStruct((spans, STATE, width), bf16),
            jax.ShapeDtypeStruct((STATE + EXTRA, width), bf16),
            jax.ShapeDtypeStruct((STATE, width), f32),
        ],
        compiler_params=params(),
        name="conv_and_states",
    )(
        group[None],
        inner_input, bc_input, bc_input, dt_input, rate,
        conv_weight_x, conv_bias_x[None], conv_weight_bc, conv_weight_bc,
        conv_bias_bc[None], conv_bias_bc[None], halo, halo, halo,
    )

    gathered = lax.all_gather(sent, "seq")

    y_local = pl.pallas_call(
        local_kernel,
        grid=(spans,),
        in_specs=[
            span_x,
            span_bc,
            span_bc,
            span_dt,
            const((heads, 1), 0, 0),
            const((1, heads), 0, 0),
            pl.BlockSpec((1, STATE, width), lambda i: (i, 0, 0)),
        ],
        out_specs=span_x,
        out_shape=jax.ShapeDtypeStruct((rows, width), f32),
        compiler_params=params(),
        cost_estimate=pl.CostEstimate(
            flops=4 * rows * width * STATE, bytes_accessed=rows * width * 8, transcendentals=0
        ),
        name="local_outputs",
    )(conv_x, conv_b, conv_c, dt_input, rate, skip_weight[None], enter)

    bits = head_count.bit_length() - 1
    distance = jnp.arange(head_count, dtype=jnp.int32) ^ head_index
    slot = jnp.zeros_like(distance)
    for bit in range(bits):
        slot = slot + ((distance >> bit) & 1) * (head_count >> (bit + 1))
    meta = jnp.concatenate([seq_index[None].astype(jnp.int32), slot.astype(jnp.int32) * block])

    normed, boundary = pl.pallas_call(
        functools.partial(output_kernel, block=block, whole_group=whole_group),
        grid_spec=pltpu.PrefetchScalarGridSpec(
            num_scalar_prefetch=1,
            grid=(spans,),
            in_specs=[
                span_x,
                span_bc,
                span_x,
                span_dt,
                const((heads, 1), 0, 0),
                const((1, width), 0, 0),
                const((seq_count, STATE + EXTRA, width), 0, 0, 0),
                const((width, STATE), 0, 0),
                const((STATE, width), 0, 0),
            ],
            out_specs=[const((rows, width), 0, 0), const((width, STATE), 0, 0)],
            scratch_shapes=[
                pltpu.VMEM((STATE, width), f32),
                pltpu.VMEM((STATE, width), bf16),
                pltpu.VMEM((SPAN, width), f32),
                pltpu.VMEM((8, heads), f32),
            ],
        ),
        out_shape=[
            jax.ShapeDtypeStruct((rows, width), bf16 if whole_group else f32),
            jax.ShapeDtypeStruct((width, STATE), f32),
        ],
        compiler_params=params(),
        name="gated_outputs",
    )(
        meta,
        y_local, conv_c, gate_input, dt_input, rate, norm_gain[None], gathered,
        init_state.reshape(width, STATE), local,
    )
    boundary = boundary.reshape(1, heads, HEADDIM, STATE)

    if not whole_group:
        piece = min(width, group_width)
        pieces = normed.reshape(rows, width // piece, piece)
        squares = jnp.sum(pieces * pieces, axis=2).T
        blocks = squares.reshape(squares.shape[0], head_count, block)
        ordered = jnp.take(blocks, slot, axis=1).reshape(squares.shape)
        own = (head_index * (width // piece) + jnp.arange(width // piece)) * piece // group_width
        member = (own[:, None] == jnp.arange(GROUPS)[None, :]).astype(f32)
        totals = lax.psum(jnp.dot(member.T, ordered, precision=highest), "head")
        sums = jnp.dot(member, totals, precision=highest)
        inverse = lax.rsqrt(sums / group_width + norm_eps)
        back = jnp.zeros_like(slot).at[slot].set(jnp.arange(head_count, dtype=slot.dtype))
        inverse = jnp.take(inverse.reshape(blocks.shape), back, axis=1).reshape(squares.shape).T
        normed = (
            (pieces * inverse[:, :, None]).reshape(rows, width) * norm_gain[None, :]
        ).astype(bf16)

    chips = seq_count // 2

    def around(value, by):
        if by % chips == 0:
            return value
        return lax.ppermute(
            value, "seq", [(i, (i + 2 * by) % seq_count) for i in range(seq_count)]
        )

    def across(value, bit):
        return lax.ppermute(
            value, "head", [(i, i ^ (1 << bit)) for i in range(head_count)]
        )

    def reduced(act, weight):
        half = rows // 2
        give = jnp.dot(act[half:], weight, preferred_element_type=f32).astype(bf16)
        keep = jnp.dot(act[:half], weight, preferred_element_type=f32)
        keep = keep + across(give, 0).astype(f32)
        for bit in range(1, bits):
            half = half // 2
            got = across(keep[half:].astype(bf16), bit)
            keep = keep[:half] + got.astype(f32)
        return keep.astype(bf16)

    core = seq_index % 2
    columns = out_weight.shape[1]
    layer_out = jnp.zeros((block, seq_count, columns), bf16)
    acts = [around(normed, by) for by in range(chips)]
    done = [[reduced(act, w) for w in (out_weight, other_core)] for act in acts]
    for by in range(chips):
        mine, other = [around(d, -by) for d in done[by]]
        chip = (seq_index // 2 + by) % chips
        layer_out = lax.dynamic_update_slice(
            layer_out, mine[:, None], (0, chip * 2 + core, 0)
        )
        layer_out = lax.dynamic_update_slice(
            layer_out, other[:, None], (0, chip * 2 + 1 - core, 0)
        )
    return (layer_out.reshape(block, seq_count * columns), boundary)


def solution(mesh):
    in_specs = (
        P("seq", "head"),
        P("seq", "head"),
        P("seq", None),
        P("head", "seq"),
        P("head"),
        P("head"),
        P(None, "head"),
        P("head"),
        P(),
        P(),
        P(None, "head"),
        P(),
        P("head", None, None),
        P("head"),
        P("head", "seq"),
    )
    out_specs = (P(("seq", "head"), None), P("seq", "head", None, None))
    return jax.shard_map(body, mesh=mesh, in_specs=in_specs, out_specs=out_specs, check_vma=False)
```

```python
import functools

import jax
import jax.numpy as jnp
from jax import lax
from jax.experimental import pallas as pl
from jax.experimental.pallas import tpu as pltpu
from jax.sharding import PartitionSpec as P

MIXER_HEADS = 256
HEADDIM = 64
STATE = 256
GROUPS = 8
KERNEL = 4
SPAN = 128
DINNER = 16384
EXTRA = 16
VMEM_LIMIT = 48 * 1024 * 1024

highest = lax.Precision.HIGHEST
norm_eps = 1e-05
f32 = jnp.float32
bf16 = jnp.bfloat16
MESH = pl.DeviceIdType.MESH


def silu(v):
    return v * (1.0 / (1.0 + jnp.exp(-v)))


def shifted(cur, prev8, by):
    moved = pltpu.roll(cur, by, 0)
    before = pltpu.roll(prev8, by, 0)
    row = lax.broadcasted_iota(jnp.int32, before.shape, 0)
    first = jnp.where(row < by, before, moved[:8])
    return jnp.concatenate([first, moved[8:]], axis=0)


def conv_block(in_ref, prev_ref, w_ref, b_ref, out_ref, chunk):
    width = in_ref.shape[1]
    rows = in_ref.shape[0]
    for c in range(0, width, chunk):
        cols = slice(c, c + chunk)
        cur = in_ref[:, cols].astype(f32)
        prev8 = prev_ref[:, cols]
        total = b_ref[:, cols] + w_ref[KERNEL - 1 : KERNEL, cols] * cur
        for by in range(1, KERNEL):
            k = KERNEL - 1 - by
            total = total + w_ref[k : k + 1, cols] * shifted(cur, prev8, by)
        prev_ref[:, cols] = cur[rows - 8 :]
        out_ref[:, cols] = silu(total).astype(bf16)


def spread_matrix(heads):
    h = lax.broadcasted_iota(jnp.int32, (heads, heads * HEADDIM), 0)
    c = lax.broadcasted_iota(jnp.int32, (heads, heads * HEADDIM), 1)
    return jnp.where(c // HEADDIM == h, 1.0, 0.0).astype(f32)


def spread(values, matrix):
    return jnp.dot(values, matrix, precision=highest, preferred_element_type=f32)


def softplus(v):
    e = jnp.exp(-jnp.abs(v))
    u = 1.0 + e
    series = e * (1.0 - e * (0.5 - e * (1.0 / 3.0 - 0.25 * e)))
    return jnp.maximum(v, 0.0) + jnp.where(e < 0.015625, series, jnp.log(u))


def transposed_dot(lhs, rhs):
    return lax.dot_general(
        lhs, rhs, (((1,), (1,)), ((), ())), precision=highest, preferred_element_type=f32
    )


def decay_terms(dt_ref, rate_ref):
    step = softplus(dt_ref[...])
    log = -jnp.exp(rate_ref[...]) * step
    t = lax.broadcasted_iota(jnp.int32, (SPAN, SPAN), 0)
    s = lax.broadcasted_iota(jnp.int32, (SPAN, SPAN), 1)
    lower = jnp.where(t >= s, 1.0, 0.0).astype(f32)
    eye = jnp.where(t == s, 1.0, 0.0).astype(f32)
    cumul_row = transposed_dot(log, lower)
    cumul_col = transposed_dot(lower, log)
    step_col = transposed_dot(eye, step)
    return step, step_col, cumul_row, cumul_col, t >= s


def state_kernel(
    g_ref, inner, bin_, cin, dt, rate, wx, bx, wb, wc, bb, bc, halo_x, halo_b, halo_c,
    x_out, b_out, c_out, enter_out, send_out, local_out,
    prev_x, prev_b, prev_c, state, total,
):
    i = pl.program_id(0)
    heads = dt.shape[0]

    @pl.when(i == 0)
    def _():
        prev_x[...] = halo_x[...].astype(f32)
        prev_b[...] = halo_b[...].astype(f32)
        prev_c[...] = halo_c[...].astype(f32)
        state[...] = jnp.zeros_like(state)
        total[...] = jnp.zeros_like(total)

    conv_block(inner, prev_x, wx, bx, x_out, 256)
    conv_block(bin_, prev_b, wb, bb, b_out, 256)
    conv_block(cin, prev_c, wc, bc, c_out, 256)
    step, step_col, cumul_row, cumul_col, causal = decay_terms(dt, rate)
    last = cumul_col[SPAN - 1 :]
    matrix = spread_matrix(heads)
    weights = spread(jnp.exp(last - cumul_col) * step_col, matrix)
    last8 = spread(jnp.broadcast_to(last, (8, heads)), matrix)
    enter_out[0] = state[...].astype(bf16)
    weighted = (x_out[...].astype(f32) * weights).astype(bf16)
    b_t = b_out[...].astype(f32).T.astype(bf16)
    written = jnp.dot(b_t, weighted, preferred_element_type=f32)
    state[...] = jnp.exp(last8[:1]) * state[...] + written
    total[...] += last8

    @pl.when(i == pl.num_programs(0) - 1)
    def _():
        local_out[...] = state[...]
        send_out[:STATE] = state[...].astype(bf16)
        tl = total[:1]
        high = tl.astype(bf16).astype(f32)
        row = lax.broadcasted_iota(jnp.int32, (EXTRA, tl.shape[1]), 0)
        send_out[STATE:] = jnp.where(row == 0, high, jnp.where(row == 1, tl - high, 0.0)).astype(bf16)


def local_kernel(x, b, c, dt, rate, skip, enter, y_out):
    heads = dt.shape[0]
    step, step_col, cumul_row, cumul_col, causal = decay_terms(dt, rate)
    matrix = spread_matrix(heads)
    scores = lax.dot_general(
        c[...], b[...], (((1,), (1,)), ((), ())), preferred_element_type=f32
    )
    row_term = jnp.log(step) - cumul_row
    growth = spread(jnp.exp(cumul_col), matrix)
    skip_row = spread(jnp.broadcast_to(skip[...], (8, heads)), matrix)[:1]
    lane = lax.broadcasted_iota(jnp.int32, (SPAN, 2 * HEADDIM), 1)
    zero = jnp.zeros((SPAN, 2 * HEADDIM), bf16)
    for pair in range(heads // 2):
        cols = slice(pair * 2 * HEADDIM, (pair + 1) * 2 * HEADDIM)
        mixers = []
        for h in (2 * pair, 2 * pair + 1):
            power = jnp.where(causal, cumul_col[:, h : h + 1] + row_term[h : h + 1], -1e30)
            mixers.append((scores * jnp.exp(power)).astype(bf16))
        xp = x[:, cols]
        both = jnp.concatenate(
            [jnp.where(lane < HEADDIM, xp, zero), jnp.where(lane >= HEADDIM, xp, zero)], axis=0
        )
        inside = jnp.dot(
            jnp.concatenate(mixers, axis=1), both, preferred_element_type=f32
        )
        carried = jnp.dot(c[...], enter[0, :, cols], preferred_element_type=f32)
        y_out[:, cols] = (
            inside + growth[:, cols] * carried + skip_row[:, cols] * xp.astype(f32)
        )


def output_kernel(
    meta, y, c, gate, dt, rate, gain, gathered, init, local, normed_out, boundary_out,
    incoming, entering, mixed, offset, *, block, whole_group,
):
    i = pl.program_id(0)
    heads = dt.shape[0]
    width = y.shape[1]
    count = gathered.shape[0]

    @pl.when(i == 0)
    def _():
        place = meta[0]
        rate_sum = jnp.zeros((1, width), f32)
        incoming[...] = jnp.zeros_like(incoming)
        for k in range(count - 2, -1, -1):
            live = k < place
            tail = gathered[k, STATE:].astype(f32)
            factor = jnp.where(live, jnp.exp(rate_sum), 0.0)
            incoming[...] += factor * gathered[k, :STATE].astype(f32)
            rate_sum = rate_sum + jnp.where(live, tail[0:1] + tail[1:2], 0.0)
        tail = gathered[place, STATE:].astype(f32)
        own = jnp.exp(tail[0:1] + tail[1:2])
        for k in range(0, width, 256):
            cols = slice(k, k + 256)
            value = incoming[:, cols] + jnp.exp(rate_sum[:, cols]) * init[cols, :].T
            entering[:, cols] = value.astype(bf16)
            boundary_out[cols, :] = (own[:, cols] * value + local[:, cols]).T
        offset[...] = jnp.zeros_like(offset)

    step, step_col, cumul_row, cumul_col, causal = decay_terms(dt, rate)
    cumul_col = cumul_col + offset[:1]
    offset[...] = jnp.broadcast_to(cumul_col[SPAN - 1 :], offset.shape)
    growth = spread(jnp.exp(cumul_col), spread_matrix(heads))
    squares = jnp.zeros((SPAN, 1), f32)
    for k in range(0, width, 256):
        cols = slice(k, k + 256)
        carried = jnp.dot(c[...], entering[:, cols], preferred_element_type=f32)
        value = (y[:, cols] + growth[:, cols] * carried) * silu(gate[:, cols].astype(f32))
        mixed[:, cols] = value
        squares = squares + jnp.sum(value * value, axis=1, keepdims=True)
    if whole_group:
        inverse = lax.rsqrt(squares / width + norm_eps)
    for q in range(SPAN // block):
        rows = slice(q * block, (q + 1) * block)
        place = pl.multiple_of(meta[1 + i * (SPAN // block) + q], block)
        value = mixed[rows, :]
        if whole_group:
            value = value * inverse[rows] * gain[...]
        normed_out[pl.ds(place, block), :] = value.astype(normed_out.dtype)


def partner_of(place, bit):
    size = 1 << bit
    return place + (1 - 2 * ((place // size) % 2)) * size


def project_kernel(
    act, w_own, w_other, out,
    w, act_x, keep, y_send, y_recv, a_send, a_recv, b_send, b_recv, x_send, x_recv,
    w_sem, act_sem, send_sem, recv_sem, x_send_sem, x_recv_sem,
):
    seq = lax.axis_index("seq")
    head = lax.axis_index("head")
    wide = w.shape[2]
    per = w_own.shape[1] // wide
    half = 2 * per
    count = 2 * half
    block = out.shape[0]
    other_chip = (seq + 2) % 4
    across = [{"head": partner_of(head, bit)} for bit in range(3)]
    over_x = {"seq": other_chip}

    def load(k, source, first):
        return pltpu.make_async_copy(
            source.at[:, pl.ds(pl.multiple_of((k - first) * wide, wide), wide)],
            w.at[k], w_sem.at[k],
        )

    def start_own(k, carry):
        load(k, w_own, 0).start()
        return carry

    def start_other(k, carry):
        load(k, w_other, per).start()
        return carry

    lax.fori_loop(0, per, start_own, 0)
    lax.fori_loop(per, half, start_other, 0)

    barrier = pltpu.get_barrier_semaphore()
    for target in across + [over_x]:
        pl.semaphore_signal(barrier, inc=1, device_id=target, device_id_type=MESH)
    pl.semaphore_wait(barrier, 4)

    def act_copy():
        return pltpu.make_async_remote_copy(
            src_ref=act, dst_ref=act_x, send_sem=act_sem.at[0], recv_sem=act_sem.at[1],
            device_id=over_x, device_id_type=MESH,
        )

    def head_copy(stage, t):
        source, target = ((y_send, y_recv), (a_send, a_recv), (b_send, b_recv))[stage]
        return pltpu.make_async_remote_copy(
            src_ref=source.at[t], dst_ref=target.at[t],
            send_sem=send_sem.at[stage, t], recv_sem=recv_sem.at[stage, t],
            device_id=across[stage], device_id_type=MESH,
        )

    def chip_copy(k):
        return pltpu.make_async_remote_copy(
            src_ref=x_send.at[k], dst_ref=x_recv.at[k],
            send_sem=x_send_sem.at[k], recv_sem=x_recv_sem.at[k],
            device_id=over_x, device_id_type=MESH,
        )

    act_copy().start()

    def multiply(source, t, k):
        y_send[t] = jnp.dot(
            source[4 * block :], w[k], preferred_element_type=f32
        ).astype(bf16)
        head_copy(0, t).start()
        keep[t] = jnp.dot(source[: 4 * block], w[k], preferred_element_type=f32)

    def column(k, home):
        core = home % 2
        return ((home // 2) * 2 + (core + k // per) % 2) * (per * wide) + (k % per) * wide

    def first_stage(t):
        head_copy(0, t).wait_recv()
        a_send[t] = (keep[t, 2 * block :] + y_recv[t, 2 * block :].astype(f32)).astype(bf16)
        head_copy(1, t).start()
        keep[t, : 2 * block] = keep[t, : 2 * block] + y_recv[t, : 2 * block].astype(f32)

    def second_stage(t):
        head_copy(1, t).wait_recv()
        b_send[t] = (keep[t, block : 2 * block] + a_recv[t, block:].astype(f32)).astype(bf16)
        head_copy(2, t).start()
        keep[t, :block] = keep[t, :block] + a_recv[t, :block].astype(f32)

    def third_stage(t):
        head_copy(2, t).wait_recv()
        return (keep[t, :block] + b_recv[t].astype(f32)).astype(bf16)

    def finish_own(t):
        out[:, pl.ds(pl.multiple_of(column(t, seq), wide), wide)] = third_stage(t)

    def finish_far(t):
        x_send[t - half] = third_stage(t)
        chip_copy(t - half).start()

    def stages(t):
        first_stage(t)

        @pl.when(t >= 1)
        def _():
            second_stage(t - 1)

        @pl.when((t >= 2) & (t < half + 2))
        def _():
            finish_own(t - 2)

        @pl.when(t >= half + 2)
        def _():
            finish_far(t - 2)

    def begin(t, carry):
        @pl.when(t < per)
        def _():
            load(t, w_own, 0).wait()

        @pl.when(t >= per)
        def _():
            load(t, w_other, per).wait()

        multiply(act, t, t)
        return carry

    ahead = 2

    def only_stages(t, carry):
        stages(t)
        return carry

    def both(t, carry):
        multiply(act_x, t + ahead, t + ahead - half)
        stages(t)
        return carry

    lax.fori_loop(0, half, begin, 0)
    lax.fori_loop(0, half - ahead, only_stages, 0)
    act_copy().wait_recv()
    lax.fori_loop(half - ahead, count - ahead, both, 0)
    lax.fori_loop(count - ahead, count, only_stages, 0)
    second_stage(count - 1)
    finish_far(count - 2)
    finish_far(count - 1)

    def collect(k, carry):
        chip_copy(k).wait_recv()
        out[:, pl.ds(pl.multiple_of(column(k, other_chip), wide), wide)] = x_recv[k]
        chip_copy(k).wait_send()
        return carry

    def drain(t, carry):
        for stage in range(3):
            head_copy(stage, t).wait_send()
        return carry

    act_copy().wait_send()
    lax.fori_loop(0, half, collect, 0)
    lax.fori_loop(0, count, drain, 0)


def project(normed, own, other):
    rows, width = normed.shape
    columns = own.shape[1]
    block = rows // 8
    wide = 512
    half = 2 * columns // wide
    count = 2 * half
    return pl.pallas_call(
        project_kernel,
        in_specs=[
            pl.BlockSpec(memory_space=pltpu.VMEM),
            pl.BlockSpec(memory_space=pl.ANY),
            pl.BlockSpec(memory_space=pl.ANY),
        ],
        out_specs=pl.BlockSpec(memory_space=pltpu.VMEM),
        out_shape=jax.ShapeDtypeStruct((block, 4 * columns), bf16),
        scratch_shapes=[
            pltpu.VMEM((half, width, wide), bf16),
            pltpu.VMEM((rows, width), bf16),
            pltpu.VMEM((count, 4 * block, wide), f32),
            pltpu.VMEM((count, 4 * block, wide), bf16),
            pltpu.VMEM((count, 4 * block, wide), bf16),
            pltpu.VMEM((count, 2 * block, wide), bf16),
            pltpu.VMEM((count, 2 * block, wide), bf16),
            pltpu.VMEM((count, block, wide), bf16),
            pltpu.VMEM((count, block, wide), bf16),
            pltpu.VMEM((half, block, wide), bf16),
            pltpu.VMEM((half, block, wide), bf16),
            pltpu.SemaphoreType.DMA((half,)),
            pltpu.SemaphoreType.DMA((2,)),
            pltpu.SemaphoreType.DMA((3, count)),
            pltpu.SemaphoreType.DMA((3, count)),
            pltpu.SemaphoreType.DMA((half,)),
            pltpu.SemaphoreType.DMA((half,)),
        ],
        compiler_params=pltpu.CompilerParams(
            vmem_limit_bytes=56 * 1024 * 1024, collective_id=0, has_side_effects=True
        ),
        name="project_and_sum",
    )(normed, own, other)


def params():
    return pltpu.CompilerParams(vmem_limit_bytes=VMEM_LIMIT)


def body(
    inner_input,
    gate_input,
    bc_input,
    dt_input,
    log_rate,
    skip_weight,
    conv_weight_x,
    conv_bias_x,
    conv_weight_bc,
    conv_bias_bc,
    conv_tail_x,
    conv_tail_bc,
    init_state,
    norm_gain,
    out_weight,
):
    seq_count = lax.axis_size("seq")
    head_count = lax.axis_size("head")
    seq_index = lax.axis_index("seq")
    head_index = lax.axis_index("head")
    rows, width = inner_input.shape
    heads = dt_input.shape[0]
    per_group = MIXER_HEADS // GROUPS
    group = (head_index * heads // per_group).astype(jnp.int32)
    spans = rows // SPAN
    block = rows // head_count
    group_width = DINNER // GROUPS
    whole_group = width == group_width

    other_core = lax.ppermute(out_weight, "seq", [(i, i ^ 1) for i in range(seq_count)])

    def pair_columns(table, axis):
        return [
            lax.dynamic_slice_in_dim(table, (g + group) * STATE, STATE, axis) for g in (0, GROUPS)
        ]

    tail_rows = rows - KERNEL + 1
    last_rows = jnp.concatenate(
        [inner_input[tail_rows:]] + pair_columns(bc_input[tail_rows:], 1), axis=1
    )
    arrived = lax.ppermute(last_rows, "seq", [(i, i + 1) for i in range(seq_count - 1)])
    first_rows = jnp.concatenate([conv_tail_x] + pair_columns(conv_tail_bc, 1), axis=1)
    halo = jnp.where(seq_index == 0, first_rows, arrived)
    halo = jnp.pad(halo, ((8 - KERNEL + 1, 0), (0, 0)))
    rate = log_rate[:, None]

    def const(shape, *index):
        return pl.BlockSpec(shape, lambda i, *_: index)

    span_x = pl.BlockSpec((SPAN, width), lambda i, *_: (i, 0))
    span_bc = pl.BlockSpec((SPAN, STATE), lambda i, *_: (i, 0))
    span_dt = pl.BlockSpec((heads, SPAN), lambda i, *_: (0, i))

    conv_x, conv_b, conv_c, enter, sent, local = pl.pallas_call(
        state_kernel,
        grid_spec=pltpu.PrefetchScalarGridSpec(
            num_scalar_prefetch=1,
            grid=(spans,),
            in_specs=[
                span_x,
                pl.BlockSpec((SPAN, STATE), lambda i, g: (i, g[0])),
                pl.BlockSpec((SPAN, STATE), lambda i, g: (i, g[0] + GROUPS)),
                span_dt,
                const((heads, 1), 0, 0),
                const((KERNEL, width), 0, 0),
                const((1, width), 0, 0),
                pl.BlockSpec((KERNEL, STATE), lambda i, g: (0, g[0])),
                pl.BlockSpec((KERNEL, STATE), lambda i, g: (0, g[0] + GROUPS)),
                pl.BlockSpec((1, STATE), lambda i, g: (0, g[0])),
                pl.BlockSpec((1, STATE), lambda i, g: (0, g[0] + GROUPS)),
                const((8, width), 0, 0),
                const((8, STATE), 0, width // STATE),
                const((8, STATE), 0, width // STATE + 1),
            ],
            out_specs=[
                span_x,
                span_bc,
                span_bc,
                pl.BlockSpec((1, STATE, width), lambda i, *_: (i, 0, 0)),
                const((STATE + EXTRA, width), 0, 0),
                const((STATE, width), 0, 0),
            ],
            scratch_shapes=[
                pltpu.VMEM((8, width), f32),
                pltpu.VMEM((8, STATE), f32),
                pltpu.VMEM((8, STATE), f32),
                pltpu.VMEM((STATE, width), f32),
                pltpu.VMEM((8, width), f32),
            ],
        ),
        out_shape=[
            jax.ShapeDtypeStruct((rows, width), bf16),
            jax.ShapeDtypeStruct((rows, STATE), bf16),
            jax.ShapeDtypeStruct((rows, STATE), bf16),
            jax.ShapeDtypeStruct((spans, STATE, width), bf16),
            jax.ShapeDtypeStruct((STATE + EXTRA, width), bf16),
            jax.ShapeDtypeStruct((STATE, width), f32),
        ],
        compiler_params=params(),
        name="conv_and_states",
    )(
        group[None],
        inner_input, bc_input, bc_input, dt_input, rate,
        conv_weight_x, conv_bias_x[None], conv_weight_bc, conv_weight_bc,
        conv_bias_bc[None], conv_bias_bc[None], halo, halo, halo,
    )

    gathered = lax.all_gather(sent, "seq")

    y_local = pl.pallas_call(
        local_kernel,
        grid=(spans,),
        in_specs=[
            span_x,
            span_bc,
            span_bc,
            span_dt,
            const((heads, 1), 0, 0),
            const((1, heads), 0, 0),
            pl.BlockSpec((1, STATE, width), lambda i: (i, 0, 0)),
        ],
        out_specs=span_x,
        out_shape=jax.ShapeDtypeStruct((rows, width), f32),
        compiler_params=params(),
        cost_estimate=pl.CostEstimate(
            flops=4 * rows * width * STATE, bytes_accessed=rows * width * 8, transcendentals=0
        ),
        name="local_outputs",
    )(conv_x, conv_b, conv_c, dt_input, rate, skip_weight[None], enter)

    bits = head_count.bit_length() - 1
    distance = jnp.arange(head_count, dtype=jnp.int32) ^ head_index
    slot = jnp.zeros_like(distance)
    for bit in range(bits):
        slot = slot + ((distance >> bit) & 1) * (head_count >> (bit + 1))
    meta = jnp.concatenate([seq_index[None].astype(jnp.int32), slot.astype(jnp.int32) * block])

    normed, boundary = pl.pallas_call(
        functools.partial(output_kernel, block=block, whole_group=whole_group),
        grid_spec=pltpu.PrefetchScalarGridSpec(
            num_scalar_prefetch=1,
            grid=(spans,),
            in_specs=[
                span_x,
                span_bc,
                span_x,
                span_dt,
                const((heads, 1), 0, 0),
                const((1, width), 0, 0),
                const((seq_count, STATE + EXTRA, width), 0, 0, 0),
                const((width, STATE), 0, 0),
                const((STATE, width), 0, 0),
            ],
            out_specs=[const((rows, width), 0, 0), const((width, STATE), 0, 0)],
            scratch_shapes=[
                pltpu.VMEM((STATE, width), f32),
                pltpu.VMEM((STATE, width), bf16),
                pltpu.VMEM((SPAN, width), f32),
                pltpu.VMEM((8, heads), f32),
            ],
        ),
        out_shape=[
            jax.ShapeDtypeStruct((rows, width), bf16 if whole_group else f32),
            jax.ShapeDtypeStruct((width, STATE), f32),
        ],
        compiler_params=params(),
        name="gated_outputs",
    )(
        meta,
        y_local, conv_c, gate_input, dt_input, rate, norm_gain[None], gathered,
        init_state.reshape(width, STATE), local,
    )
    boundary = boundary.reshape(1, heads, HEADDIM, STATE)

    if not whole_group:
        piece = min(width, group_width)
        pieces = normed.reshape(rows, width // piece, piece)
        squares = jnp.sum(pieces * pieces, axis=2).T
        blocks = squares.reshape(squares.shape[0], head_count, block)
        ordered = jnp.take(blocks, slot, axis=1).reshape(squares.shape)
        own = (head_index * (width // piece) + jnp.arange(width // piece)) * piece // group_width
        member = (own[:, None] == jnp.arange(GROUPS)[None, :]).astype(f32)
        totals = lax.psum(jnp.dot(member.T, ordered, precision=highest), "head")
        sums = jnp.dot(member, totals, precision=highest)
        inverse = lax.rsqrt(sums / group_width + norm_eps)
        back = jnp.zeros_like(slot).at[slot].set(jnp.arange(head_count, dtype=slot.dtype))
        inverse = jnp.take(inverse.reshape(blocks.shape), back, axis=1).reshape(squares.shape).T
        normed = (
            (pieces * inverse[:, :, None]).reshape(rows, width) * norm_gain[None, :]
        ).astype(bf16)

    if seq_count == 4 and head_count == 8 and whole_group and out_weight.shape[1] % 512 == 0:
        return (project(normed, out_weight, other_core), boundary)

    chips = seq_count // 2

    def around(value, by):
        if by % chips == 0:
            return value
        return lax.ppermute(
            value, "seq", [(i, (i + 2 * by) % seq_count) for i in range(seq_count)]
        )

    def across(value, bit):
        return lax.ppermute(
            value, "head", [(i, i ^ (1 << bit)) for i in range(head_count)]
        )

    def reduced(act, weight):
        half = rows // 2
        give = jnp.dot(act[half:], weight, preferred_element_type=f32).astype(bf16)
        keep = jnp.dot(act[:half], weight, preferred_element_type=f32)
        keep = keep + across(give, 0).astype(f32)
        for bit in range(1, bits):
            half = half // 2
            got = across(keep[half:].astype(bf16), bit)
            keep = keep[:half] + got.astype(f32)
        return keep.astype(bf16)

    core = seq_index % 2
    columns = out_weight.shape[1]
    layer_out = jnp.zeros((block, seq_count, columns), bf16)
    acts = [around(normed, by) for by in range(chips)]
    done = [[reduced(act, w) for w in (out_weight, other_core)] for act in acts]
    for by in range(chips):
        mine, other = [around(d, -by) for d in done[by]]
        chip = (seq_index // 2 + by) % chips
        layer_out = lax.dynamic_update_slice(
            layer_out, mine[:, None], (0, chip * 2 + core, 0)
        )
        layer_out = lax.dynamic_update_slice(
            layer_out, other[:, None], (0, chip * 2 + 1 - core, 0)
        )
    return (layer_out.reshape(block, seq_count * columns), boundary)


def solution(mesh):
    in_specs = (
        P("seq", "head"),
        P("seq", "head"),
        P("seq", None),
        P("head", "seq"),
        P("head"),
        P("head"),
        P(None, "head"),
        P("head"),
        P(),
        P(),
        P(None, "head"),
        P(),
        P("head", None, None),
        P("head"),
        P("head", "seq"),
    )
    out_specs = (P(("seq", "head"), None), P("seq", "head", None, None))
    return jax.shard_map(body, mesh=mesh, in_specs=in_specs, out_specs=out_specs, check_vma=False)
```

```python
import functools

import jax
import jax.numpy as jnp
from jax import lax
from jax.experimental import pallas as pl
from jax.experimental.pallas import tpu as pltpu
from jax.sharding import PartitionSpec as P

MIXER_HEADS = 256
HEADDIM = 64
STATE = 256
GROUPS = 8
KERNEL = 4
SPAN = 128
DINNER = 16384
EXTRA = 16
VMEM_LIMIT = 48 * 1024 * 1024

highest = lax.Precision.HIGHEST
norm_eps = 1e-05
f32 = jnp.float32
bf16 = jnp.bfloat16
MESH = pl.DeviceIdType.MESH


def silu(v):
    return v * (1.0 / (1.0 + jnp.exp(-v)))


def shifted(cur, prev8, by):
    moved = pltpu.roll(cur, by, 0)
    before = pltpu.roll(prev8, by, 0)
    row = lax.broadcasted_iota(jnp.int32, before.shape, 0)
    first = jnp.where(row < by, before, moved[:8])
    return jnp.concatenate([first, moved[8:]], axis=0)


def conv_block(in_ref, prev_ref, w_ref, b_ref, out_ref, chunk):
    width = in_ref.shape[1]
    rows = in_ref.shape[0]
    for c in range(0, width, chunk):
        cols = slice(c, c + chunk)
        cur = in_ref[:, cols].astype(f32)
        prev8 = prev_ref[:, cols]
        total = b_ref[:, cols] + w_ref[KERNEL - 1 : KERNEL, cols] * cur
        for by in range(1, KERNEL):
            k = KERNEL - 1 - by
            total = total + w_ref[k : k + 1, cols] * shifted(cur, prev8, by)
        prev_ref[:, cols] = cur[rows - 8 :]
        out_ref[:, cols] = silu(total).astype(bf16)


def spread_matrix(heads):
    h = lax.broadcasted_iota(jnp.int32, (heads, heads * HEADDIM), 0)
    c = lax.broadcasted_iota(jnp.int32, (heads, heads * HEADDIM), 1)
    return jnp.where(c // HEADDIM == h, 1.0, 0.0).astype(f32)


def spread(values, matrix):
    return jnp.dot(values, matrix, precision=highest, preferred_element_type=f32)


def softplus(v):
    e = jnp.exp(-jnp.abs(v))
    u = 1.0 + e
    series = e * (1.0 - e * (0.5 - e * (1.0 / 3.0 - 0.25 * e)))
    return jnp.maximum(v, 0.0) + jnp.where(e < 0.015625, series, jnp.log(u))


def transposed_dot(lhs, rhs):
    return lax.dot_general(
        lhs, rhs, (((1,), (1,)), ((), ())), precision=highest, preferred_element_type=f32
    )


def decay_terms(dt_ref, rate_ref):
    step = softplus(dt_ref[...])
    log = -jnp.exp(rate_ref[...]) * step
    t = lax.broadcasted_iota(jnp.int32, (SPAN, SPAN), 0)
    s = lax.broadcasted_iota(jnp.int32, (SPAN, SPAN), 1)
    lower = jnp.where(t >= s, 1.0, 0.0).astype(f32)
    eye = jnp.where(t == s, 1.0, 0.0).astype(f32)
    cumul_row = transposed_dot(log, lower)
    cumul_col = transposed_dot(lower, log)
    step_col = transposed_dot(eye, step)
    return step, step_col, cumul_row, cumul_col, t >= s


def state_kernel(
    g_ref, inner, bin_, cin, dt, rate, wx, bx, wb, wc, bb, bc, halo_x, halo_b, halo_c,
    x_out, b_out, c_out, enter_out, send_out, local_out,
    prev_x, prev_b, prev_c, state, total,
):
    i = pl.program_id(0)
    heads = dt.shape[0]

    @pl.when(i == 0)
    def _():
        prev_x[...] = halo_x[...].astype(f32)
        prev_b[...] = halo_b[...].astype(f32)
        prev_c[...] = halo_c[...].astype(f32)
        state[...] = jnp.zeros_like(state)
        total[...] = jnp.zeros_like(total)

    conv_block(inner, prev_x, wx, bx, x_out, 256)
    conv_block(bin_, prev_b, wb, bb, b_out, 256)
    conv_block(cin, prev_c, wc, bc, c_out, 256)
    step, step_col, cumul_row, cumul_col, causal = decay_terms(dt, rate)
    last = cumul_col[SPAN - 1 :]
    matrix = spread_matrix(heads)
    weights = spread(jnp.exp(last - cumul_col) * step_col, matrix)
    last8 = spread(jnp.broadcast_to(last, (8, heads)), matrix)
    enter_out[0] = state[...].astype(bf16)
    weighted = (x_out[...].astype(f32) * weights).astype(bf16)
    b_t = b_out[...].astype(f32).T.astype(bf16)
    written = jnp.dot(b_t, weighted, preferred_element_type=f32)
    state[...] = jnp.exp(last8[:1]) * state[...] + written
    total[...] += last8

    @pl.when(i == pl.num_programs(0) - 1)
    def _():
        local_out[...] = state[...]
        send_out[:STATE] = state[...].astype(bf16)
        tl = total[:1]
        high = tl.astype(bf16).astype(f32)
        row = lax.broadcasted_iota(jnp.int32, (EXTRA, tl.shape[1]), 0)
        send_out[STATE:] = jnp.where(row == 0, high, jnp.where(row == 1, tl - high, 0.0)).astype(bf16)


PARTS = 4


def chain_kernel(
    x, b, c, dt, rate, skip, enter, local, sent, y_out, prior_out,
    land, hop, send_sem, recv_sem,
):
    i = pl.program_id(0)
    seq = lax.axis_index("seq")
    last = 3
    wide = land.shape[2]

    def copy(k):
        return pltpu.make_async_remote_copy(
            src_ref=hop.at[k], dst_ref=land.at[k],
            send_sem=send_sem.at[k], recv_sem=recv_sem.at[k],
            device_id={"seq": (seq + 1) % 4}, device_id_type=MESH,
        )

    def joined(k):
        cols = slice(k * wide, (k + 1) * wide)
        own = sent[STATE : STATE + 1, cols].astype(f32) + sent[STATE + 1 : STATE + 2, cols].astype(f32)
        tail = land[k, STATE:].astype(f32)
        hop[k, :STATE] = (
            jnp.exp(own) * land[k, :STATE].astype(f32) + local[:, cols]
        ).astype(bf16)
        log = tail[0:1] + tail[1:2] + own
        high = log.astype(bf16).astype(f32)
        row = lax.broadcasted_iota(jnp.int32, (EXTRA, wide), 0)
        hop[k, STATE:] = jnp.where(row == 0, high, jnp.where(row == 1, log - high, 0.0)).astype(bf16)

    @pl.when(i == 0)
    def _():
        barrier = pltpu.get_barrier_semaphore()

        for by in (1, 3):
            pl.semaphore_signal(
                barrier, inc=1, device_id={"seq": (seq + by) % 4}, device_id_type=MESH
            )
        pl.semaphore_wait(barrier, 2)

        @pl.when(seq == 0)
        def _():
            for k in range(PARTS):
                hop[k] = sent[:, k * wide : (k + 1) * wide]
                copy(k).start()

        @pl.when(seq == 1)
        def _():
            for k in range(PARTS):
                copy(k).wait_recv()
                joined(k)
                copy(k).start()

    local_kernel(x, b, c, dt, rate, skip, enter, y_out)

    @pl.when(i == pl.num_programs(0) - 1)
    def _():
        @pl.when(seq == 2)
        def _():
            for k in range(PARTS):
                copy(k).wait_recv()
                joined(k)
                copy(k).start()

        @pl.when(seq == 3)
        def _():
            for k in range(PARTS):
                copy(k).wait_recv()

        @pl.when(seq > 0)
        def _():
            for k in range(PARTS):
                prior_out[:, k * wide : (k + 1) * wide] = land[k]

        @pl.when(seq == 0)
        def _():
            prior_out[...] = jnp.zeros_like(prior_out)

        @pl.when(seq < last)
        def _():
            for k in range(PARTS):
                copy(k).wait_send()


def local_kernel(x, b, c, dt, rate, skip, enter, y_out):
    heads = dt.shape[0]
    step, step_col, cumul_row, cumul_col, causal = decay_terms(dt, rate)
    matrix = spread_matrix(heads)
    scores = lax.dot_general(
        c[...], b[...], (((1,), (1,)), ((), ())), preferred_element_type=f32
    )
    row_term = jnp.log(step) - cumul_row
    growth = spread(jnp.exp(cumul_col), matrix)
    skip_row = spread(jnp.broadcast_to(skip[...], (8, heads)), matrix)[:1]
    lane = lax.broadcasted_iota(jnp.int32, (SPAN, 2 * HEADDIM), 1)
    zero = jnp.zeros((SPAN, 2 * HEADDIM), bf16)
    for pair in range(heads // 2):
        cols = slice(pair * 2 * HEADDIM, (pair + 1) * 2 * HEADDIM)
        mixers = []
        for h in (2 * pair, 2 * pair + 1):
            power = jnp.where(causal, cumul_col[:, h : h + 1] + row_term[h : h + 1], -1e30)
            mixers.append((scores * jnp.exp(power)).astype(bf16))
        xp = x[:, cols]
        both = jnp.concatenate(
            [jnp.where(lane < HEADDIM, xp, zero), jnp.where(lane >= HEADDIM, xp, zero)], axis=0
        )
        inside = jnp.dot(
            jnp.concatenate(mixers, axis=1), both, preferred_element_type=f32
        )
        carried = jnp.dot(c[...], enter[0, :, cols], preferred_element_type=f32)
        y_out[:, cols] = (
            inside + growth[:, cols] * carried + skip_row[:, cols] * xp.astype(f32)
        )


def output_kernel(
    meta, y, c, gate, dt, rate, gain, gathered, own_tail, init, local, normed_out, boundary_out,
    incoming, entering, mixed, offset, *, block, whole_group, chained,
):
    i = pl.program_id(0)
    heads = dt.shape[0]
    width = y.shape[1]
    count = gathered.shape[0]

    @pl.when(i == 0)
    def _():
        place = meta[0]
        rate_sum = jnp.zeros((1, width), f32)
        incoming[...] = jnp.zeros_like(incoming)
        if chained:
            tail = gathered[0, STATE:].astype(f32)
            incoming[...] = gathered[0, :STATE].astype(f32)
            rate_sum = tail[0:1] + tail[1:2]
        for k in range(-1 if chained else count - 2, -1, -1):
            live = k < place
            tail = gathered[k, STATE:].astype(f32)
            factor = jnp.where(live, jnp.exp(rate_sum), 0.0)
            incoming[...] += factor * gathered[k, :STATE].astype(f32)
            rate_sum = rate_sum + jnp.where(live, tail[0:1] + tail[1:2], 0.0)
        tail = (own_tail[...] if chained else gathered[place, STATE:]).astype(f32)
        own = jnp.exp(tail[0:1] + tail[1:2])
        for k in range(0, width, 256):
            cols = slice(k, k + 256)
            value = incoming[:, cols] + jnp.exp(rate_sum[:, cols]) * init[cols, :].T
            entering[:, cols] = value.astype(bf16)
            boundary_out[cols, :] = (own[:, cols] * value + local[:, cols]).T
        offset[...] = jnp.zeros_like(offset)

    step, step_col, cumul_row, cumul_col, causal = decay_terms(dt, rate)
    cumul_col = cumul_col + offset[:1]
    offset[...] = jnp.broadcast_to(cumul_col[SPAN - 1 :], offset.shape)
    growth = spread(jnp.exp(cumul_col), spread_matrix(heads))
    squares = jnp.zeros((SPAN, 1), f32)
    for k in range(0, width, 256):
        cols = slice(k, k + 256)
        carried = jnp.dot(c[...], entering[:, cols], preferred_element_type=f32)
        value = (y[:, cols] + growth[:, cols] * carried) * silu(gate[:, cols].astype(f32))
        mixed[:, cols] = value
        squares = squares + jnp.sum(value * value, axis=1, keepdims=True)
    if whole_group:
        inverse = lax.rsqrt(squares / width + norm_eps)
    for q in range(SPAN // block):
        rows = slice(q * block, (q + 1) * block)
        place = pl.multiple_of(meta[1 + i * (SPAN // block) + q], block)
        value = mixed[rows, :]
        if whole_group:
            value = value * inverse[rows] * gain[...]
        normed_out[pl.ds(place, block), :] = value.astype(normed_out.dtype)


def partner_of(place, bit):
    size = 1 << bit
    return place + (1 - 2 * ((place // size) % 2)) * size


def project_kernel(
    act, w_own, w_other, out,
    w, acts, act_x, keep, y_send, y_recv, a_send, a_recv, b_send, b_recv, x_send, x_recv,
    w_sem, act_sem, send_sem, recv_sem, x_send_sem, x_recv_sem,
):
    seq = lax.axis_index("seq")
    head = lax.axis_index("head")
    wide = w.shape[2]
    per = w_own.shape[1] // wide
    half = 2 * per
    count = 2 * half
    block = out.shape[0]
    other_chip = (seq + 2) % 4
    near = [partner_of(head, bit) for bit in range(3)]
    across = [{"head": place} for place in near]

    def turned(t):
        return (t % 4) // 3

    def target_of(stage, t):
        if stage == 2:
            return across[2]
        return {"head": near[stage] + turned(t) * (near[1 - stage] - near[stage])}

    def reorder(source, dest):
        for part, first in enumerate((0, 4, 2, 6)):
            dest[part * 2 * block : (part + 1) * 2 * block] = source[
                first * block : (first + 2) * block
            ]

    over_x = {"seq": other_chip}

    def load(k, source, first):
        return pltpu.make_async_copy(
            source.at[:, pl.ds(pl.multiple_of((k - first) * wide, wide), wide)],
            w.at[k], w_sem.at[k],
        )

    def start_own(k, carry):
        load(k, w_own, 0).start()
        return carry

    def start_other(k, carry):
        load(k, w_other, per).start()
        return carry

    lax.fori_loop(0, per, start_own, 0)
    lax.fori_loop(per, half, start_other, 0)

    barrier = pltpu.get_barrier_semaphore()
    for target in across + [over_x]:
        pl.semaphore_signal(barrier, inc=1, device_id=target, device_id_type=MESH)
    pl.semaphore_wait(barrier, 4)

    def act_copy():
        return pltpu.make_async_remote_copy(
            src_ref=act, dst_ref=act_x.at[0], send_sem=act_sem.at[0], recv_sem=act_sem.at[1],
            device_id=over_x, device_id_type=MESH,
        )

    def head_copy(stage, t):
        source, target = ((y_send, y_recv), (a_send, a_recv), (b_send, b_recv))[stage]
        return pltpu.make_async_remote_copy(
            src_ref=source.at[t], dst_ref=target.at[t],
            send_sem=send_sem.at[stage, t], recv_sem=recv_sem.at[stage, t],
            device_id=target_of(stage, t), device_id_type=MESH,
        )

    def chip_copy(k):
        return pltpu.make_async_remote_copy(
            src_ref=x_send.at[k], dst_ref=x_recv.at[k],
            send_sem=x_send_sem.at[k], recv_sem=x_recv_sem.at[k],
            device_id=over_x, device_id_type=MESH,
        )

    act_copy().start()
    acts[0] = act[...]
    reorder(act, acts.at[1])

    def multiply(source, t, k):
        slot = turned(t)
        y_send[t] = jnp.dot(
            source[slot, 4 * block :], w[k], preferred_element_type=f32
        ).astype(bf16)
        head_copy(0, t).start()
        keep[t] = jnp.dot(source[slot, : 4 * block], w[k], preferred_element_type=f32)

    def column(k, home):
        core = home % 2
        return ((home // 2) * 2 + (core + k // per) % 2) * (per * wide) + (k % per) * wide

    def first_stage(t):
        head_copy(0, t).wait_recv()
        a_send[t] = (keep[t, 2 * block :] + y_recv[t, 2 * block :].astype(f32)).astype(bf16)
        head_copy(1, t).start()
        keep[t, : 2 * block] = keep[t, : 2 * block] + y_recv[t, : 2 * block].astype(f32)

    def second_stage(t):
        head_copy(1, t).wait_recv()
        b_send[t] = (keep[t, block : 2 * block] + a_recv[t, block:].astype(f32)).astype(bf16)
        head_copy(2, t).start()
        keep[t, :block] = keep[t, :block] + a_recv[t, :block].astype(f32)

    def third_stage(t):
        head_copy(2, t).wait_recv()
        return (keep[t, :block] + b_recv[t].astype(f32)).astype(bf16)

    def finish_own(t):
        out[:, pl.ds(pl.multiple_of(column(t, seq), wide), wide)] = third_stage(t)

    def finish_far(t):
        x_send[t - half] = third_stage(t)
        chip_copy(t - half).start()

    def stages(t):
        first_stage(t)

        @pl.when(t >= 1)
        def _():
            second_stage(t - 1)

        @pl.when((t >= 2) & (t < half + 2))
        def _():
            finish_own(t - 2)

        @pl.when(t >= half + 2)
        def _():
            finish_far(t - 2)

    def begin(t, carry):
        @pl.when(t < per)
        def _():
            load(t, w_own, 0).wait()

        @pl.when(t >= per)
        def _():
            load(t, w_other, per).wait()

        multiply(acts, t, t)
        return carry

    ahead = 2

    def only_stages(t, carry):
        stages(t)
        return carry

    def both(t, carry):
        multiply(act_x, t + ahead, t + ahead - half)
        stages(t)
        return carry

    lax.fori_loop(0, half, begin, 0)
    lax.fori_loop(0, half - ahead, only_stages, 0)
    act_copy().wait_recv()
    reorder(act_x.at[0], act_x.at[1])
    lax.fori_loop(half - ahead, count - ahead, both, 0)
    lax.fori_loop(count - ahead, count, only_stages, 0)
    second_stage(count - 1)
    finish_far(count - 2)
    finish_far(count - 1)

    def collect(k, carry):
        chip_copy(k).wait_recv()
        out[:, pl.ds(pl.multiple_of(column(k, other_chip), wide), wide)] = x_recv[k]
        chip_copy(k).wait_send()
        return carry

    def drain(t, carry):
        for stage in range(3):
            head_copy(stage, t).wait_send()
        return carry

    act_copy().wait_send()
    lax.fori_loop(0, half, collect, 0)
    lax.fori_loop(0, count, drain, 0)


def project(normed, own, other):
    rows, width = normed.shape
    columns = own.shape[1]
    block = rows // 8
    wide = 512
    half = 2 * columns // wide
    count = 2 * half
    return pl.pallas_call(
        project_kernel,
        in_specs=[
            pl.BlockSpec(memory_space=pltpu.VMEM),
            pl.BlockSpec(memory_space=pl.ANY),
            pl.BlockSpec(memory_space=pl.ANY),
        ],
        out_specs=pl.BlockSpec(memory_space=pltpu.VMEM),
        out_shape=jax.ShapeDtypeStruct((block, 4 * columns), bf16),
        scratch_shapes=[
            pltpu.VMEM((half, width, wide), bf16),
            pltpu.VMEM((2, rows, width), bf16),
            pltpu.VMEM((2, rows, width), bf16),
            pltpu.VMEM((count, 4 * block, wide), f32),
            pltpu.VMEM((count, 4 * block, wide), bf16),
            pltpu.VMEM((count, 4 * block, wide), bf16),
            pltpu.VMEM((count, 2 * block, wide), bf16),
            pltpu.VMEM((count, 2 * block, wide), bf16),
            pltpu.VMEM((count, block, wide), bf16),
            pltpu.VMEM((count, block, wide), bf16),
            pltpu.VMEM((half, block, wide), bf16),
            pltpu.VMEM((half, block, wide), bf16),
            pltpu.SemaphoreType.DMA((half,)),
            pltpu.SemaphoreType.DMA((2,)),
            pltpu.SemaphoreType.DMA((3, count)),
            pltpu.SemaphoreType.DMA((3, count)),
            pltpu.SemaphoreType.DMA((half,)),
            pltpu.SemaphoreType.DMA((half,)),
        ],
        compiler_params=pltpu.CompilerParams(
            vmem_limit_bytes=56 * 1024 * 1024, collective_id=0, has_side_effects=True
        ),
        name="project_and_sum",
    )(normed, own, other)


def params():
    return pltpu.CompilerParams(vmem_limit_bytes=VMEM_LIMIT)


def body(
    inner_input,
    gate_input,
    bc_input,
    dt_input,
    log_rate,
    skip_weight,
    conv_weight_x,
    conv_bias_x,
    conv_weight_bc,
    conv_bias_bc,
    conv_tail_x,
    conv_tail_bc,
    init_state,
    norm_gain,
    out_weight,
):
    seq_count = lax.axis_size("seq")
    head_count = lax.axis_size("head")
    seq_index = lax.axis_index("seq")
    head_index = lax.axis_index("head")
    rows, width = inner_input.shape
    heads = dt_input.shape[0]
    per_group = MIXER_HEADS // GROUPS
    group = (head_index * heads // per_group).astype(jnp.int32)
    spans = rows // SPAN
    block = rows // head_count
    group_width = DINNER // GROUPS
    whole_group = width == group_width

    other_core = lax.ppermute(out_weight, "seq", [(i, i ^ 1) for i in range(seq_count)])

    def pair_columns(table, axis):
        return [
            lax.dynamic_slice_in_dim(table, (g + group) * STATE, STATE, axis) for g in (0, GROUPS)
        ]

    tail_rows = rows - KERNEL + 1
    last_rows = jnp.concatenate(
        [inner_input[tail_rows:]] + pair_columns(bc_input[tail_rows:], 1), axis=1
    )
    arrived = lax.ppermute(last_rows, "seq", [(i, i + 1) for i in range(seq_count - 1)])
    first_rows = jnp.concatenate([conv_tail_x] + pair_columns(conv_tail_bc, 1), axis=1)
    halo = jnp.where(seq_index == 0, first_rows, arrived)
    halo = jnp.pad(halo, ((8 - KERNEL + 1, 0), (0, 0)))
    rate = log_rate[:, None]

    def const(shape, *index):
        return pl.BlockSpec(shape, lambda i, *_: index)

    span_x = pl.BlockSpec((SPAN, width), lambda i, *_: (i, 0))
    span_bc = pl.BlockSpec((SPAN, STATE), lambda i, *_: (i, 0))
    span_dt = pl.BlockSpec((heads, SPAN), lambda i, *_: (0, i))

    conv_x, conv_b, conv_c, enter, sent, local = pl.pallas_call(
        state_kernel,
        grid_spec=pltpu.PrefetchScalarGridSpec(
            num_scalar_prefetch=1,
            grid=(spans,),
            in_specs=[
                span_x,
                pl.BlockSpec((SPAN, STATE), lambda i, g: (i, g[0])),
                pl.BlockSpec((SPAN, STATE), lambda i, g: (i, g[0] + GROUPS)),
                span_dt,
                const((heads, 1), 0, 0),
                const((KERNEL, width), 0, 0),
                const((1, width), 0, 0),
                pl.BlockSpec((KERNEL, STATE), lambda i, g: (0, g[0])),
                pl.BlockSpec((KERNEL, STATE), lambda i, g: (0, g[0] + GROUPS)),
                pl.BlockSpec((1, STATE), lambda i, g: (0, g[0])),
                pl.BlockSpec((1, STATE), lambda i, g: (0, g[0] + GROUPS)),
                const((8, width), 0, 0),
                const((8, STATE), 0, width // STATE),
                const((8, STATE), 0, width // STATE + 1),
            ],
            out_specs=[
                span_x,
                span_bc,
                span_bc,
                pl.BlockSpec((1, STATE, width), lambda i, *_: (i, 0, 0)),
                const((STATE + EXTRA, width), 0, 0),
                const((STATE, width), 0, 0),
            ],
            scratch_shapes=[
                pltpu.VMEM((8, width), f32),
                pltpu.VMEM((8, STATE), f32),
                pltpu.VMEM((8, STATE), f32),
                pltpu.VMEM((STATE, width), f32),
                pltpu.VMEM((8, width), f32),
            ],
        ),
        out_shape=[
            jax.ShapeDtypeStruct((rows, width), bf16),
            jax.ShapeDtypeStruct((rows, STATE), bf16),
            jax.ShapeDtypeStruct((rows, STATE), bf16),
            jax.ShapeDtypeStruct((spans, STATE, width), bf16),
            jax.ShapeDtypeStruct((STATE + EXTRA, width), bf16),
            jax.ShapeDtypeStruct((STATE, width), f32),
        ],
        compiler_params=params(),
        name="conv_and_states",
    )(
        group[None],
        inner_input, bc_input, bc_input, dt_input, rate,
        conv_weight_x, conv_bias_x[None], conv_weight_bc, conv_weight_bc,
        conv_bias_bc[None], conv_bias_bc[None], halo, halo, halo,
    )

    chained = seq_count == 4 and width % (PARTS * 128) == 0
    local_specs = [
        span_x,
        span_bc,
        span_bc,
        span_dt,
        const((heads, 1), 0, 0),
        const((1, heads), 0, 0),
        pl.BlockSpec((1, STATE, width), lambda i: (i, 0, 0)),
    ]
    local_args = (conv_x, conv_b, conv_c, dt_input, rate, skip_weight[None], enter)
    y_shape = jax.ShapeDtypeStruct((rows, width), f32)
    if chained:
        slots = (PARTS, STATE + EXTRA, width // PARTS)
        y_local, prior = pl.pallas_call(
            chain_kernel,
            grid=(spans,),
            in_specs=local_specs
            + [const((STATE, width), 0, 0), const((STATE + EXTRA, width), 0, 0)],
            out_specs=[span_x, const((STATE + EXTRA, width), 0, 0)],
            out_shape=[y_shape, jax.ShapeDtypeStruct((STATE + EXTRA, width), bf16)],
            scratch_shapes=[
                pltpu.VMEM(slots, bf16),
                pltpu.VMEM(slots, bf16),
                pltpu.SemaphoreType.DMA((PARTS,)),
                pltpu.SemaphoreType.DMA((PARTS,)),
            ],
            compiler_params=pltpu.CompilerParams(
                vmem_limit_bytes=VMEM_LIMIT, collective_id=1, has_side_effects=True
            ),
            name="local_outputs_and_chain",
        )(*local_args, local, sent)
        gathered = prior[None]
    else:
        gathered = lax.all_gather(sent, "seq")
        y_local = pl.pallas_call(
            local_kernel,
            grid=(spans,),
            in_specs=local_specs,
            out_specs=span_x,
            out_shape=y_shape,
            compiler_params=params(),
            name="local_outputs",
        )(*local_args)

    bits = head_count.bit_length() - 1
    distance = jnp.arange(head_count, dtype=jnp.int32) ^ head_index
    slot = jnp.zeros_like(distance)
    for bit in range(bits):
        slot = slot + ((distance >> bit) & 1) * (head_count >> (bit + 1))
    meta = jnp.concatenate([seq_index[None].astype(jnp.int32), slot.astype(jnp.int32) * block])

    normed, boundary = pl.pallas_call(
        functools.partial(
            output_kernel, block=block, whole_group=whole_group, chained=chained
        ),
        grid_spec=pltpu.PrefetchScalarGridSpec(
            num_scalar_prefetch=1,
            grid=(spans,),
            in_specs=[
                span_x,
                span_bc,
                span_x,
                span_dt,
                const((heads, 1), 0, 0),
                const((1, width), 0, 0),
                const((gathered.shape[0], STATE + EXTRA, width), 0, 0, 0),
                const((EXTRA, width), STATE // EXTRA, 0),
                const((width, STATE), 0, 0),
                const((STATE, width), 0, 0),
            ],
            out_specs=[const((rows, width), 0, 0), const((width, STATE), 0, 0)],
            scratch_shapes=[
                pltpu.VMEM((STATE, width), f32),
                pltpu.VMEM((STATE, width), bf16),
                pltpu.VMEM((SPAN, width), f32),
                pltpu.VMEM((8, heads), f32),
            ],
        ),
        out_shape=[
            jax.ShapeDtypeStruct((rows, width), bf16 if whole_group else f32),
            jax.ShapeDtypeStruct((width, STATE), f32),
        ],
        compiler_params=params(),
        name="gated_outputs",
    )(
        meta,
        y_local, conv_c, gate_input, dt_input, rate, norm_gain[None], gathered, sent,
        init_state.reshape(width, STATE), local,
    )
    boundary = boundary.reshape(1, heads, HEADDIM, STATE)

    if not whole_group:
        piece = min(width, group_width)
        pieces = normed.reshape(rows, width // piece, piece)
        squares = jnp.sum(pieces * pieces, axis=2).T
        blocks = squares.reshape(squares.shape[0], head_count, block)
        ordered = jnp.take(blocks, slot, axis=1).reshape(squares.shape)
        own = (head_index * (width // piece) + jnp.arange(width // piece)) * piece // group_width
        member = (own[:, None] == jnp.arange(GROUPS)[None, :]).astype(f32)
        totals = lax.psum(jnp.dot(member.T, ordered, precision=highest), "head")
        sums = jnp.dot(member, totals, precision=highest)
        inverse = lax.rsqrt(sums / group_width + norm_eps)
        back = jnp.zeros_like(slot).at[slot].set(jnp.arange(head_count, dtype=slot.dtype))
        inverse = jnp.take(inverse.reshape(blocks.shape), back, axis=1).reshape(squares.shape).T
        normed = (
            (pieces * inverse[:, :, None]).reshape(rows, width) * norm_gain[None, :]
        ).astype(bf16)

    if seq_count == 4 and head_count == 8 and whole_group and out_weight.shape[1] % 512 == 0:
        return (project(normed, out_weight, other_core), boundary)

    chips = seq_count // 2

    def around(value, by):
        if by % chips == 0:
            return value
        return lax.ppermute(
            value, "seq", [(i, (i + 2 * by) % seq_count) for i in range(seq_count)]
        )

    def across(value, bit):
        return lax.ppermute(
            value, "head", [(i, i ^ (1 << bit)) for i in range(head_count)]
        )

    def reduced(act, weight):
        half = rows // 2
        give = jnp.dot(act[half:], weight, preferred_element_type=f32).astype(bf16)
        keep = jnp.dot(act[:half], weight, preferred_element_type=f32)
        keep = keep + across(give, 0).astype(f32)
        for bit in range(1, bits):
            half = half // 2
            got = across(keep[half:].astype(bf16), bit)
            keep = keep[:half] + got.astype(f32)
        return keep.astype(bf16)

    core = seq_index % 2
    columns = out_weight.shape[1]
    layer_out = jnp.zeros((block, seq_count, columns), bf16)
    acts = [around(normed, by) for by in range(chips)]
    done = [[reduced(act, w) for w in (out_weight, other_core)] for act in acts]
    for by in range(chips):
        mine, other = [around(d, -by) for d in done[by]]
        chip = (seq_index // 2 + by) % chips
        layer_out = lax.dynamic_update_slice(
            layer_out, mine[:, None], (0, chip * 2 + core, 0)
        )
        layer_out = lax.dynamic_update_slice(
            layer_out, other[:, None], (0, chip * 2 + 1 - core, 0)
        )
    return (layer_out.reshape(block, seq_count * columns), boundary)


def solution(mesh):
    in_specs = (
        P("seq", "head"),
        P("seq", "head"),
        P("seq", None),
        P("head", "seq"),
        P("head"),
        P("head"),
        P(None, "head"),
        P("head"),
        P(),
        P(),
        P(None, "head"),
        P(),
        P("head", None, None),
        P("head"),
        P("head", "seq"),
    )
    out_specs = (P(("seq", "head"), None), P("seq", "head", None, None))
    return jax.shard_map(body, mesh=mesh, in_specs=in_specs, out_specs=out_specs, check_vma=False)
```
